256 devices in a mesh: grp: 16 (over z, core), sib: 16 (over y, x).
Axes of the slice: x: 4, y: 4, z: 8, core: 2. Of those that a mesh axis runs over, the one named last changes fastest.
Arguments:
- targets: float32 [327680, 256], P(('grp', 'sib')), may hold values from -6 to 6
- leaf_order: int32 [256, 1280], P(('grp', 'sib')), may hold values from 0 to 1279, each once within a row
- near_block: float32 [327680, 1280], P(('grp', 'sib')), may hold values from -0.15625 to 0.15625
- leaf_basis: float32 [327680, 128], P(('grp', 'sib')), may hold values from -0.15625 to 0.15625
- sibling_coupling: float32 [32768, 2048], P(('grp', 'sib')), may hold values from -0.5 to 0.5
- transfer: float32 [32768, 128], P(('grp', 'sib')), may hold values from -0.5 to 0.5
- top_coupling: float32 [2048, 2048], P('grp', 'sib'), may hold values from -0.125 to 0.125
Outputs:
- coefficients: float32 [327680, 256], P(('grp', 'sib'))
- fitted: float32 [327680, 256], P(('grp', 'sib'))
The draws below stay inside these ranges and needn't reach their ends.
Inputs may be any that keep to these rules, and one draw needn't show every extreme that they name: `leaf_order`: each row of 1280 entries holds every number of 0 to 1279 once.
All inputs are finite; a program needn't handle non-finite values.
Results may differ from the reference program's by a relative error of at most 0.00025.
Values sent between devices are 32-bit elements; how exact they have to be, the bound alone decides.
No kernel may reach another device: no remote copies, remote signals or barrier semaphores. Data moves between devices by JAX's collectives and lax.ppermute only.
A program may use at most 64 MiB of HBM per device.

```python
import jax
import jax.numpy as jnp
from jax import lax

LEAF = 1280
COUPLING_RANK = 128
TARGET_COLUMNS = 256
ITERS = 3
POINTS = 327680
N_GRP = 16
N_SIB = 16
DEVICES = 256


def level_of(own_key, shape, cuts, smallest, high):
    def one(dim, parts):
        draws = jax.random.uniform(jax.random.fold_in(jax.random.fold_in(own_key, 6), dim), (parts,), jnp.float32, smallest / len(cuts), high / len(cuts))
        return jnp.repeat(jnp.exp(draws), shape[dim] // parts).reshape((-1,) + (1,) * (len(shape) - dim - 1))

    factor_of = one(*cuts[0])
    for cut in cuts[1:]:
        factor_of = factor_of * one(*cut)
    return factor_of


def gaussian(own_key, dims, scale, bound, pieces=(), held_as=jnp.bfloat16):
    drawn = jax.random.normal(own_key, dims, jnp.float32) * scale
    if len(pieces) > 0:
        drawn = level_of(own_key, dims, pieces, -0.22, 0.18) * drawn
    return jnp.clip(drawn, min=-bound, max=bound).astype(held_as)


def setup_inputs(seed: int = 0) -> dict:
    arg_keys = jax.random.split(jax.random.key(seed), 8)
    return {
        "targets": gaussian(arg_keys[0], (POINTS, TARGET_COLUMNS), 1.0, 6.0, ((0, 256),), jnp.float32),
        "leaf_order": jax.vmap(lambda own: jax.random.permutation(own, LEAF))(jax.random.split(arg_keys[1], DEVICES)).reshape((DEVICES, LEAF)).astype(jnp.int32),
        "near_block": gaussian(arg_keys[2], (POINTS, LEAF), LEAF ** -0.5, 0.15625, ((0, 256),), jnp.float32),
        "leaf_basis": gaussian(arg_keys[3], (POINTS, COUPLING_RANK), LEAF ** -0.5, 0.15625, ((0, 256),), jnp.float32),
        "sibling_coupling": gaussian(arg_keys[4], (DEVICES * COUPLING_RANK, N_SIB * COUPLING_RANK), COUPLING_RANK ** -0.5, 0.5, ((0, 256),), jnp.float32),
        "transfer": gaussian(arg_keys[5], (DEVICES * COUPLING_RANK, COUPLING_RANK), COUPLING_RANK ** -0.5, 0.5, ((0, 256),), jnp.float32),
        "top_coupling": gaussian(arg_keys[6], (N_GRP * COUPLING_RANK, N_GRP * COUPLING_RANK), (N_GRP * COUPLING_RANK) ** -0.5, 0.125, ((0, 16), (1, 16)), jnp.float32),
    }


step_size = 0.5
shrink_rate = 0.1
highest_level = lax.Precision.HIGHEST


def reference(targets, leaf_order, near_block, leaf_basis, sibling_coupling, transfer, top_coupling):
    ordering = leaf_order.reshape(DEVICES, LEAF).astype(jnp.int32)
    leaf_targets = targets.reshape(DEVICES, LEAF, TARGET_COLUMNS)
    tree_targets = jnp.take_along_axis(leaf_targets, ordering[:, :, None], axis=1)
    nearby_blocks = near_block.reshape(DEVICES, LEAF, LEAF)
    nested_basis = leaf_basis.reshape(DEVICES, LEAF, COUPLING_RANK)
    sib_mask = 1.0 - jnp.eye(N_SIB, dtype=jnp.float32)
    sibling = sibling_coupling.reshape(N_GRP, N_SIB, COUPLING_RANK, N_SIB, COUPLING_RANK) * sib_mask[None, :, None, :, None]
    upward_pass = transfer.reshape(N_GRP, N_SIB, COUPLING_RANK, COUPLING_RANK)
    grp_mask = 1.0 - jnp.eye(N_GRP, dtype=jnp.float32)
    root_level = top_coupling.reshape(N_GRP, COUPLING_RANK, N_GRP, COUPLING_RANK) * grp_mask[:, None, :, None]

    def apply_kernel(weight_coefficients):
        nearby_part = jnp.einsum('yac,ycf->yaf', nearby_blocks, weight_coefficients, precision=highest_level)
        leaf_coefficients = jnp.einsum('ojq,ojv->oqv', nested_basis, weight_coefficients, precision=highest_level).reshape(N_GRP, N_SIB, COUPLING_RANK, TARGET_COLUMNS)
        sibling_sum = jnp.einsum('gsrkq,gkqt->gsrt', sibling, leaf_coefficients, precision=highest_level)
        cluster_coefficient = jnp.einsum('cyma,cymd->cad', upward_pass, leaf_coefficients, precision=highest_level)
        root_sum = jnp.einsum('pizc,zce->pie', root_level, cluster_coefficient, precision=highest_level)
        downward_pass = sibling_sum + jnp.einsum('gsrq,gqt->gsrt', upward_pass, root_sum, precision=highest_level)
        distant_part = jnp.einsum('lsy,lyj->lsj', nested_basis, downward_pass.reshape(DEVICES, COUPLING_RANK, TARGET_COLUMNS), precision=highest_level)
        return nearby_part + distant_part

    weight_coefficients = step_size * tree_targets
    fitted = weight_coefficients
    for iteration in range(ITERS):
        fitted = jnp.tanh(apply_kernel(weight_coefficients))
        weight_coefficients = weight_coefficients + step_size * (tree_targets - fitted) - step_size * shrink_rate * weight_coefficients
    leaves = jnp.arange(DEVICES).astype(jnp.int32)[:, None]
    coeffs_out = jnp.zeros_like(weight_coefficients).at[leaves, ordering].set(weight_coefficients)
    fitted_out = jnp.zeros_like(fitted).at[leaves, ordering].set(fitted)
    return coeffs_out.reshape(POINTS, TARGET_COLUMNS), fitted_out.reshape(POINTS, TARGET_COLUMNS)
```

```python
import functools
import math

import jax
import jax.numpy as jnp
from jax import lax
from jax.experimental import pallas as pl
from jax.experimental.pallas import tpu as pltpu
from jax.sharding import PartitionSpec as P


ITERS = 3
SIDE = 4
TILE = 256
VMEM_GRANT = 34 << 20

step_size = 0.5
shrink_rate = 0.1
f32, bf16 = jnp.float32, jnp.bfloat16


def halves(value):
    high = value.astype(bf16)
    return high, (value - high.astype(f32)).astype(bf16)


def product(left, right):
    dot = functools.partial(jnp.dot, preferred_element_type=f32)
    return dot(left[0], right[0]) + (dot(left[0], right[1]) + dot(left[1], right[0]))


def call(kernel, outs, flops, *args, near_by=0, **kwargs):
    far = len(args) - near_by
    moved = sum(v.size * v.dtype.itemsize for v in args)
    moved += sum(math.prod(shape) * jnp.dtype(kind).itemsize for shape, kind in outs)
    outs = [pltpu.HBM(*out) for out in outs]
    args = [pltpu.with_memory_space_constraint(v, pltpu.HBM) for v in args[:far]] + [*args[far:]]
    return pl.pallas_call(
        kernel,
        out_shape=outs,
        cost_estimate=pl.CostEstimate(flops=flops, bytes_accessed=moved, transcendentals=0),
        compiler_params=pltpu.CompilerParams(vmem_limit_bytes=VMEM_GRANT),
        **kwargs,
    )(*args)


def exchange(copies, axis):
    return lax.all_to_all(copies, axis, split_axis=0, concat_axis=0, tiled=True)


def shifted(value, rows, columns):
    pairs = [
        (r * SIDE + c, (r + rows) % SIDE * SIDE + (c + columns) % SIDE)
        for r in range(SIDE)
        for c in range(SIDE)
    ]
    return lax.ppermute(value, "sib", pairs)


def sibling_behind(rows, columns):
    sib = lax.axis_index("sib")
    row = lax.rem(sib // SIDE + SIDE - rows, SIDE)
    return row * SIDE + lax.rem(sib % SIDE + SIDE - columns, SIDE)


def arrange_kernel(row_ref, top_ref, own_ref, *sent_refs):
    rank = row_ref.shape[0]
    for ahead in range(SIDE):
        target = own_ref if ahead == 0 else sent_refs[ahead - 1]
        for behind in range(SIDE):
            spot = slice(behind * rank, (behind + 1) * rank)
            if ahead == 0 and behind == 0:
                target[:, spot] = jnp.zeros((rank, rank), f32)
            else:
                source = sibling_behind(SIDE - ahead, behind) if ahead else sibling_behind(0, behind)
                target[:, spot] = row_ref[:, pl.ds(pl.multiple_of(source * rank, rank), rank)]
        if ahead:
            target[:, SIDE * rank :] = top_ref[...]


def arrange(sibling_row, top_block):
    rank = top_block.shape[0]
    wide = ((rank, (SIDE + 1) * rank), f32)
    outs = [((rank, SIDE * rank), f32)] + [wide] * (SIDE - 1)
    return call(arrange_kernel, outs, 0, sibling_row, top_block)


def couple_kernel(top_ref, own_ref, *refs):
    *got, split_ref, tops_ref = refs
    rank = top_ref.shape[0]
    tops_ref[0] = top_ref[...]
    for above in range(SIDE):
        rows = slice(above * rank, (above + 1) * rank)
        block = own_ref[...] if above == 0 else got[above - 1][:, : SIDE * rank]
        split_ref[0, rows, :], split_ref[1, rows, :] = halves(block)
        if above:
            tops_ref[above] = got[above - 1][:, SIDE * rank :]


def couple(top_block, own, got):
    rank = top_block.shape[0]
    outs = [((2, SIDE * rank, SIDE * rank), bf16), ((SIDE, rank, rank), f32)]
    return call(couple_kernel, outs, 0, top_block, own, *got, near_by=SIDE - 1)


def place_kernel(*refs):
    *parts, out_ref = refs
    for behind in range(SIDE):
        for above in range(SIDE):
            owner = sibling_behind(above, behind)
            out_ref[0, owner], out_ref[1, owner] = halves(parts[behind][above].T)


def place(parts):
    _, rank, width = parts[0].shape
    return call(place_kernel, [((2, SIDE * SIDE, rank, width), bf16)], 0, *parts, near_by=SIDE - 1)[0]


def bands(rows):
    return rows // TILE


def band(index):
    return pl.ds(pl.multiple_of(index * TILE, TILE), TILE)


def over_bands(rows, body):
    lax.fori_loop(0, bands(rows), lambda k, _: body(k), None)


def copies_of(*ends):
    return [pltpu.make_async_copy(*end) for end in ends]


def start(copies):
    for copy in copies:
        copy.start()
    return copies


def finish(copies):
    for copy in copies:
        copy.wait()


def banded(pairs, sems, index):
    cut = band(index)
    return copies_of(*((a.at[cut], b.at[cut], sems.at[n, index]) for n, (a, b) in enumerate(pairs)))


def add_up(total_ref, basis, weights):
    dot = functools.partial(
        lax.dot_general, dimension_numbers=(((0,), (0,)), ((), ())), preferred_element_type=f32
    )
    part = dot(basis[0], weights[0]) + (dot(basis[0], weights[1]) + dot(basis[1], weights[0]))
    total_ref[...] += part


def send_up(total_ref, leaf, group, leaf_ref, group_ref, sems):
    rank = leaf.shape[0]
    leaf[...] = total_ref[:rank, :]
    group[...] = total_ref[rank:, :].T
    return start(copies_of((leaf, leaf_ref, sems.at[0]), (group, group_ref, sems.at[1])))


HBM = pl.BlockSpec(memory_space=pltpu.HBM)
VMEM = pl.BlockSpec(memory_space=pltpu.VMEM)
DMA = pltpu.SemaphoreType.DMA


def begin_kernel(targets_ref, basis_ref, transfer_ref, *refs):
    split_ref, leaf_ref, group_ref, targets, basis, split, total, leaf, group, *sems = refs
    in_sems, out_sems, end_sems = sems
    rows = basis.shape[0]
    pairs = ((targets_ref, targets), (basis_ref, basis))
    outgoing = ((split.at[0], split_ref.at[0]), (split.at[1], split_ref.at[1]))
    over_bands(rows, lambda k: (start(banded(pairs, in_sems, k)), None)[1])
    transfer = halves(transfer_ref[...])
    total[...] = jnp.zeros_like(total)

    def step(k):
        cut = band(k)
        finish(banded(pairs, in_sems, k))
        both = jnp.concatenate([basis[cut, :], product(halves(basis[cut, :]), transfer)], axis=1)
        high, low = halves(both)
        split[0, cut, :] = high
        split[1, cut, :] = low
        start(banded(outgoing, out_sems, k))
        add_up(total, (high, low), halves(step_size * targets[cut, :]))

    over_bands(rows, step)
    sent = send_up(total, leaf, group, leaf_ref, group_ref, end_sems)
    over_bands(rows, lambda k: finish(banded(outgoing, out_sems, k)))
    finish(sent)


def begin(tree_targets, basis, transfer):
    rows, columns = tree_targets.shape
    rank = transfer.shape[0]
    outs = [((2, rows, 2 * rank), bf16), ((rank, columns), f32), ((columns, rank), f32)]
    return call(
        begin_kernel,
        outs,
        18 * rows * columns * rank,
        tree_targets,
        basis,
        transfer,
        in_specs=[HBM, HBM, VMEM],
        near_by=1,
        out_specs=[HBM] * 3,
        scratch_shapes=[
            pltpu.VMEM((rows, columns), f32),
            pltpu.VMEM((rows, rank), f32),
            pltpu.VMEM(*outs[0]),
            pltpu.VMEM((2 * rank, columns), f32),
            *(pltpu.VMEM(*out) for out in outs[1:]),
            DMA((2, bands(rows))),
            DMA((2, bands(rows))),
            DMA((2,)),
        ],
    )


def fit_kernel(last, *refs):
    sum_ref, base_ref, along_ref, root_ref, *refs = refs
    if last:
        order_ref, coeffs_ref, fitted_ref, sums, base, along, split, in_sems, out_sems = refs
        outgoing = ((sums, coeffs_ref), (base, fitted_ref))
    else:
        coeffs_ref, leaf_ref, group_ref, sums, base, along, *refs = refs
        total, leaf, group, in_sems, out_sems, end_sems = refs
        total[...] = jnp.zeros_like(total)
        outgoing = ((base, coeffs_ref),)
    rows, columns = sums.shape
    rank = root_ref.shape[1]
    pairs = ((sum_ref, sums), (base_ref, base))
    pairs += ((along_ref.at[0], along.at[0]), (along_ref.at[1], along.at[1]))
    over_bands(rows, lambda k: (start(banded(pairs, in_sems, k)), None)[1])
    root = halves(root_ref[...].T)

    def step(k):
        cut = band(k)
        finish(banded(pairs, in_sems, k))
        high, low = along[0, cut, :], along[1, cut, :]
        fitted = jnp.tanh(sums[cut, :] + product((along[0, cut, rank:], along[1, cut, rank:]), root))
        weights = base[cut, :] - step_size * fitted
        if last:
            for n, part in enumerate((*halves(weights), *halves(fitted))):
                split[cut, n * columns : (n + 1) * columns] = part
        else:
            base[cut, :] = weights
            start(banded(outgoing, out_sems, k))
            add_up(total, (high, low), halves(weights))

    over_bands(rows, step)
    if last:
        order = order_ref[...]

        def scatter(k):
            cut = band(k)
            positions = lax.broadcasted_iota(jnp.int32, (TILE, rows), 0) + k * TILE
            chosen = jnp.where(positions == order, 1.0, 0.0).astype(bf16)
            parts = jnp.dot(chosen, split[...], preferred_element_type=f32)
            sums[cut, :] = parts[:, :columns] + parts[:, columns : 2 * columns]
            base[cut, :] = parts[:, 2 * columns : 3 * columns] + parts[:, 3 * columns :]
            start(banded(outgoing, out_sems, k))

        over_bands(rows, scatter)
    else:
        sent = send_up(total, leaf, group, leaf_ref, group_ref, end_sems)
        finish(sent)
    over_bands(rows, lambda k: finish(banded(outgoing, out_sems, k)))


def fit(last, sums, base, along, root, order):
    rows, columns = sums.shape
    rank = root.shape[1]
    state = ((rows, columns), f32)
    scratch = [pltpu.VMEM(*state)] * 2 + [pltpu.VMEM(along.shape, bf16)]
    sems = [DMA((4, bands(rows))), DMA((2, bands(rows)))]
    if last:
        outs = [state, state]
        scratch += [pltpu.VMEM((rows, 4 * columns), bf16)]
    else:
        outs = [state, ((rank, columns), f32), ((columns, rank), f32)]
        scratch += [pltpu.VMEM((2 * rank, columns), f32)]
        scratch += [pltpu.VMEM(*out) for out in outs[1:]]
        sems += [DMA((2,))]
    return call(
        functools.partial(fit_kernel, last),
        outs,
        18 * rows * columns * rank,
        sums,
        base,
        along,
        root,
        *((order,) if last else ()),
        in_specs=[HBM] * 3 + [VMEM] * (2 if last else 1),
        near_by=2 if last else 1,
        out_specs=[HBM] * len(outs),
        scratch_shapes=scratch + sems,
    )


def near_kernel(first, *refs):
    old_ref, *refs = refs
    given, refs = refs[: 1 if first else 2], refs[1 if first else 2 :]
    along_ref, *refs = refs
    siblings, refs = refs[:SIDE], refs[SIDE:]
    sum_ref, base_ref, *refs = refs
    if first:
        split_ref, block, *refs = refs
    old, sums, base, leaf, split, ready, *refs = refs
    if not first:
        now, *refs = refs
    in_sems, out_sems, start_sems = refs
    rank = siblings[0].shape[0]
    rows = sums.shape[0]
    outgoing = ((sums, sum_ref), (base, base_ref))
    if first:
        arrived = copies_of((old_ref, old, start_sems.at[0]))
        pairs = ((given[0], block),)
        outgoing += ((split.at[0], split_ref.at[0]), (split.at[1], split_ref.at[1]))
    else:
        arrived = copies_of((given[0], now, start_sems.at[0]))
        pairs = ((given[1].at[0], split.at[0]), (given[1].at[1], split.at[1]), (old_ref, old))
    arrived += copies_of((along_ref.at[:, :, pl.ds(0, rank)], leaf, start_sems.at[1]))
    start(arrived)
    over_bands(rows, lambda k: (start(banded(pairs, in_sems, k)), None)[1])
    total = siblings[0][...]
    for ref in siblings[1:]:
        total = total + ref[...]
    total = halves(total)
    finish(arrived)
    ready[0], ready[1] = halves(step_size * old[...] if first else now[...])

    def step(k):
        cut = band(k)
        finish(banded(pairs, in_sems, k))
        if first:
            split[0, cut, :], split[1, cut, :] = halves(block[cut, :])
        weights = step_size * old[cut, :] if first else now[cut, :]
        near = product((split[0, cut, :], split[1, cut, :]), (ready[0], ready[1]))
        sums[cut, :] = near + product((leaf[0, cut, :], leaf[1, cut, :]), total)
        base[cut, :] = weights - step_size * shrink_rate * weights + step_size * old[cut, :]
        start(banded(outgoing, out_sems, k))

    over_bands(rows, step)
    over_bands(rows, lambda k: finish(banded(outgoing, out_sems, k)))


def near_sum(blocks, weights, targets, along, siblings):
    rows, columns = targets.shape
    rank = siblings[0].shape[0]
    first = weights is None
    state = ((rows, columns), f32)
    split = ((2, rows, rows), bf16)
    shapes = [((rows, rows), f32)] if first else []
    shapes += [state] * 3 + [((2, rows, rank), bf16), split, ((2, rows, columns), bf16)]
    shapes += [] if first else [state]
    return call(
        functools.partial(near_kernel, first),
        [state] * 2 + ([split] if first else []),
        6 * rows * rows * columns,
        targets,
        *(() if first else (weights,)),
        blocks,
        along,
        *siblings,
        in_specs=[HBM] * (3 if first else 4) + [VMEM] * SIDE,
        near_by=SIDE - 1,
        out_specs=[HBM] * (3 if first else 2),
        scratch_shapes=[pltpu.VMEM(*shape) for shape in shapes]
        + [DMA((3, bands(rows))), DMA((4, bands(rows))), DMA((2,))],
    )


def sibling_kernel(split_ref, *refs):
    parts, (first_ref, *out_refs) = refs[:SIDE], refs[SIDE : 2 * SIDE]
    split, sums, in_sem, out_sems = refs[2 * SIDE :]
    rank = parts[0].shape[0]
    arriving = start(copies_of((split_ref, split, in_sem)))
    coefficients = halves(jnp.concatenate([ref[...] for ref in parts]))
    finish(arriving)
    sums[...] = product((split[0], split[1]), coefficients)
    outs = enumerate(out_refs, 1)
    sent = start(
        copies_of(*((sums.at[pl.ds(k * rank, rank)], out, out_sems.at[k - 1]) for k, out in outs))
    )
    first_ref[...] = sums[:rank, :]
    finish(sent)


def sibling_sums(couplings, parts):
    rank, columns = parts[0].shape
    return call(
        sibling_kernel,
        [((rank, columns), f32)] * SIDE,
        6 * SIDE * SIDE * rank * rank * columns,
        couplings,
        *parts,
        in_specs=[HBM] + [VMEM] * SIDE,
        near_by=SIDE - 1,
        out_specs=[VMEM] + [HBM] * (SIDE - 1),
        scratch_shapes=[
            pltpu.VMEM(couplings.shape, bf16),
            pltpu.VMEM((SIDE * rank, columns), f32),
            DMA(()),
            DMA((SIDE - 1,)),
        ],
    )


def sum_kernel(parts_ref, out_ref):
    total = parts_ref[0]
    for k in range(1, parts_ref.shape[0]):
        total = total + parts_ref[k]
    for k in range(out_ref.shape[0]):
        out_ref[k] = total
    out_ref[lax.axis_index("grp")] = jnp.zeros_like(total)


def sum_copies(parts):
    length = lax.axis_size("grp")
    return call(sum_kernel, [((length, *parts.shape[1:]), f32)], 0, parts, near_by=1)[0]


def root_kernel(split_ref, parts_ref, out_ref):
    groups, _, rank = parts_ref.shape
    parts = jnp.concatenate([parts_ref[k] for k in range(groups)], axis=1)
    couplings = [split_ref[k].reshape(groups * rank, rank) for k in range(2)]
    root = product(halves(parts), couplings)
    for k in range(out_ref.shape[0]):
        out_ref[k] = root


def root_copies(parts, tops):
    groups, share, rank = parts.shape
    outs = [((lax.axis_size("sib"), share, rank), f32)]
    return call(root_kernel, outs, 6 * groups * share * rank * rank, tops, parts, near_by=1)[0]


def shards(targets, leaf_order, near_block, leaf_basis, sibling_coupling, transfer, top_coupling):
    ordering = leaf_order[0]
    _, columns = targets.shape
    rank = transfer.shape[0]
    sibs = lax.axis_size("sib")
    share = columns // sibs
    tree_targets = targets.at[ordering].get(unique_indices=True, mode="promise_in_bounds")
    along, leaf_part, group_part = begin(tree_targets, leaf_basis, transfer)
    own, *sent = arrange(sibling_coupling, top_coupling)
    got = [shifted(block, ahead, 0) for ahead, block in enumerate(sent, 1)]
    row_couplings, top_blocks = couple(top_coupling, own, got)
    blocks = near_block
    weights = None
    for iteration in range(ITERS):
        last = iteration == ITERS - 1
        arrived = exchange(group_part.reshape(sibs, share, rank), "sib")
        parts = [leaf_part] + [shifted(leaf_part, 0, behind) for behind in range(1, SIDE)]
        if iteration == 0:
            tops = [top_blocks] + [shifted(top_blocks, 0, behind) for behind in range(1, SIDE)]
            tops = place(tops)
        group_copies = sum_copies(arrived)
        others = exchange(group_copies, "grp")
        sums = sibling_sums(row_couplings, parts)
        sums = [sums[0]] + [shifted(sums[ahead], -ahead, 0) for ahead in range(1, SIDE)]
        roots = root_copies(others, tops)
        root_whole = exchange(roots, "sib").reshape(columns, rank)
        near, base, *split = near_sum(blocks, weights, tree_targets, along, sums)
        blocks = split[0] if split else blocks
        outs = fit(last, near, base, along, root_whole, leaf_order)
        if not last:
            weights, leaf_part, group_part = outs
    return tuple(outs)


def solution(mesh):
    split = P(("grp", "sib"), None)
    return jax.shard_map(
        shards,
        mesh=mesh,
        in_specs=(split,) * 6 + (P("grp", "sib"),),
        out_specs=(split, split),
        check_vma=False,
    )
```

```python
import functools
import math

import jax
import jax.numpy as jnp
from jax import lax
from jax.experimental import pallas as pl
from jax.experimental.pallas import tpu as pltpu
from jax.sharding import PartitionSpec as P


ITERS = 3
SIDE = 4
TILE = 256
WIDE = 640
AHEAD = 2
VMEM_GRANT = 34 << 20

step_size = 0.5
shrink_rate = 0.1
f32, bf16 = jnp.float32, jnp.bfloat16


def halves(value):
    high = value.astype(bf16)
    return high, (value - high.astype(f32)).astype(bf16)


def product(left, right):
    dot = functools.partial(jnp.dot, preferred_element_type=f32)
    return dot(left[0], right[0]) + (dot(left[0], right[1]) + dot(left[1], right[0]))


def call(kernel, outs, flops, *args, near_by=0, **kwargs):
    far = len(args) - near_by
    moved = sum(v.size * v.dtype.itemsize for v in args)
    moved += sum(math.prod(shape) * jnp.dtype(kind).itemsize for shape, kind in outs)
    outs = [pltpu.HBM(*out) for out in outs]
    args = [pltpu.with_memory_space_constraint(v, pltpu.HBM) for v in args[:far]] + [*args[far:]]
    return pl.pallas_call(
        kernel,
        out_shape=outs,
        cost_estimate=pl.CostEstimate(flops=flops, bytes_accessed=moved, transcendentals=0),
        compiler_params=pltpu.CompilerParams(vmem_limit_bytes=VMEM_GRANT),
        **kwargs,
    )(*args)


def exchange(copies, axis):
    return lax.all_to_all(copies, axis, split_axis=0, concat_axis=0, tiled=True)


def shifted(value, rows, columns):
    pairs = [
        (r * SIDE + c, (r + rows) % SIDE * SIDE + (c + columns) % SIDE)
        for r in range(SIDE)
        for c in range(SIDE)
    ]
    return lax.ppermute(value, "sib", pairs)


def sibling_behind(rows, columns):
    sib = lax.axis_index("sib")
    row = lax.rem(sib // SIDE + SIDE - rows, SIDE)
    return row * SIDE + lax.rem(sib % SIDE + SIDE - columns, SIDE)


def arrange_kernel(row_ref, top_ref, own_ref, *sent_refs):
    rank = row_ref.shape[0]
    for ahead in range(SIDE):
        target = own_ref if ahead == 0 else sent_refs[ahead - 1]
        for behind in range(SIDE):
            spot = slice(behind * rank, (behind + 1) * rank)
            if ahead == 0 and behind == 0:
                target[:, spot] = jnp.zeros((rank, rank), f32)
            else:
                source = sibling_behind(SIDE - ahead, behind) if ahead else sibling_behind(0, behind)
                target[:, spot] = row_ref[:, pl.ds(pl.multiple_of(source * rank, rank), rank)]
        if ahead:
            target[:, SIDE * rank :] = top_ref[...]


def arrange(sibling_row, top_block):
    rank = top_block.shape[0]
    wide = ((rank, (SIDE + 1) * rank), f32)
    outs = [((rank, SIDE * rank), f32)] + [wide] * (SIDE - 1)
    return call(arrange_kernel, outs, 0, sibling_row, top_block)


def couple_kernel(top_ref, own_ref, *refs):
    *got, split_ref, tops_ref = refs
    rank = top_ref.shape[0]
    tops_ref[0] = top_ref[...]
    for above in range(SIDE):
        rows = slice(above * rank, (above + 1) * rank)
        block = own_ref[...] if above == 0 else got[above - 1][:, : SIDE * rank]
        split_ref[0, rows, :], split_ref[1, rows, :] = halves(block)
        if above:
            tops_ref[above] = got[above - 1][:, SIDE * rank :]


def couple(top_block, own, got):
    rank = top_block.shape[0]
    outs = [((2, SIDE * rank, SIDE * rank), bf16), ((SIDE, rank, rank), f32)]
    return call(couple_kernel, outs, 0, top_block, own, *got, near_by=SIDE - 1)


def place_kernel(*refs):
    *parts, out_ref = refs
    for behind in range(SIDE):
        for above in range(SIDE):
            owner = sibling_behind(above, behind)
            out_ref[0, owner], out_ref[1, owner] = halves(parts[behind][above].T)


def place(parts):
    _, rank, width = parts[0].shape
    return call(place_kernel, [((2, SIDE * SIDE, rank, width), bf16)], 0, *parts, near_by=SIDE - 1)[0]


def band(index, tile):
    return pl.ds(pl.multiple_of(index * tile, tile), tile)


def over_bands(count, body):
    lax.fori_loop(0, count, lambda k, _: body(k), None)


def copies_of(*ends):
    return [pltpu.make_async_copy(*end) for end in ends]


def start(copies):
    for copy in copies:
        copy.start()
    return copies


def finish(copies):
    for copy in copies:
        copy.wait()


def banded(pairs, sems, index):
    tile = pairs[0][0].shape[0] // sems.shape[1]
    cut = band(index, tile)
    return copies_of(*((a.at[cut], b.at[cut], sems.at[n, index]) for n, (a, b) in enumerate(pairs)))


def lead(pairs, sems):
    for k in range(min(AHEAD, sems.shape[1])):
        start(banded(pairs, sems, k))


def stream(pairs, sems, body, ahead=AHEAD):
    def step(k):
        @pl.when(k + ahead < sems.shape[1])
        def _():
            start(banded(pairs, sems, k + ahead))

        finish(banded(pairs, sems, k))
        body(k)

    over_bands(sems.shape[1], step)


def add_up(total_ref, basis, weights):
    dot = functools.partial(
        lax.dot_general, dimension_numbers=(((0,), (0,)), ((), ())), preferred_element_type=f32
    )
    part = dot(basis[0], weights[0]) + (dot(basis[0], weights[1]) + dot(basis[1], weights[0]))
    total_ref[...] += part


def send_up(total_ref, leaf, group, leaf_ref, group_ref, sems):
    rank = leaf.shape[0]
    leaf[...] = total_ref[:rank, :]
    group[...] = total_ref[rank:, :].T
    return start(copies_of((leaf, leaf_ref, sems.at[0]), (group, group_ref, sems.at[1])))


HBM = pl.BlockSpec(memory_space=pltpu.HBM)
VMEM = pl.BlockSpec(memory_space=pltpu.VMEM)
DMA = pltpu.SemaphoreType.DMA


def begin_kernel(targets_ref, basis_ref, transfer_ref, *refs):
    split_ref, leaf_ref, group_ref, targets, basis, split, total, leaf, group, *sems = refs
    in_sems, out_sems, end_sems = sems
    rows = basis.shape[0]
    pairs = ((targets_ref, targets), (basis_ref, basis))
    outgoing = ((split.at[0], split_ref.at[0]), (split.at[1], split_ref.at[1]))
    lead(pairs, in_sems)
    transfer = halves(transfer_ref[...])
    total[...] = jnp.zeros_like(total)

    def step(k):
        cut = band(k, WIDE)
        both = jnp.concatenate([basis[cut, :], product(halves(basis[cut, :]), transfer)], axis=1)
        high, low = halves(both)
        split[0, cut, :] = high
        split[1, cut, :] = low
        start(banded(outgoing, out_sems, k))
        add_up(total, (high, low), halves(step_size * targets[cut, :]))

    stream(pairs, in_sems, step)
    sent = send_up(total, leaf, group, leaf_ref, group_ref, end_sems)
    over_bands(rows // WIDE, lambda k: finish(banded(outgoing, out_sems, k)))
    finish(sent)


def begin(tree_targets, basis, transfer):
    rows, columns = tree_targets.shape
    rank = transfer.shape[0]
    outs = [((2, rows, 2 * rank), bf16), ((rank, columns), f32), ((columns, rank), f32)]
    return call(
        begin_kernel,
        outs,
        18 * rows * columns * rank,
        tree_targets,
        basis,
        transfer,
        in_specs=[HBM, HBM, VMEM],
        near_by=1,
        out_specs=[HBM] * 3,
        scratch_shapes=[
            pltpu.VMEM((rows, columns), f32),
            pltpu.VMEM((rows, rank), f32),
            pltpu.VMEM(*outs[0]),
            pltpu.VMEM((2 * rank, columns), f32),
            *(pltpu.VMEM(*out) for out in outs[1:]),
            DMA((2, rows // WIDE)),
            DMA((2, rows // WIDE)),
            DMA((2,)),
        ],
    )


def fit_kernel(last, *refs):
    sum_ref, base_ref, along_ref, root_ref, *refs = refs
    if last:
        order_ref, coeffs_ref, fitted_ref, sums, base, along, split, in_sems, out_sems = refs
        outgoing = ((sums, coeffs_ref), (base, fitted_ref))
    else:
        coeffs_ref, leaf_ref, group_ref, sums, base, along, *refs = refs
        total, leaf, group, in_sems, out_sems, end_sems = refs
        total[...] = jnp.zeros_like(total)
        outgoing = ((base, coeffs_ref),)
    rows, columns = sums.shape
    rank = root_ref.shape[1]
    pairs = ((sum_ref, sums), (base_ref, base))
    pairs += ((along_ref.at[0], along.at[0]), (along_ref.at[1], along.at[1]))
    lead(pairs, in_sems)
    root = halves(root_ref[...].T)

    def step(k):
        cut = band(k, WIDE)
        high, low = along[0, cut, :], along[1, cut, :]
        fitted = jnp.tanh(sums[cut, :] + product((along[0, cut, rank:], along[1, cut, rank:]), root))
        weights = base[cut, :] - step_size * fitted
        if last:
            for n, part in enumerate((*halves(weights), *halves(fitted))):
                split[cut, n * columns : (n + 1) * columns] = part
        else:
            base[cut, :] = weights
            start(banded(outgoing, out_sems, k))
            add_up(total, (high, low), halves(weights))

    stream(pairs, in_sems, step)
    if last:
        order = order_ref[...]

        def scatter(k):
            cut = band(k, WIDE)
            positions = lax.broadcasted_iota(jnp.int32, (WIDE, rows), 0) + k * WIDE
            chosen = jnp.where(positions == order, 1.0, 0.0).astype(bf16)
            parts = jnp.dot(chosen, split[...], preferred_element_type=f32)
            sums[cut, :] = parts[:, :columns] + parts[:, columns : 2 * columns]
            base[cut, :] = parts[:, 2 * columns : 3 * columns] + parts[:, 3 * columns :]
            start(banded(outgoing, out_sems, k))

        over_bands(rows // WIDE, scatter)
    else:
        sent = send_up(total, leaf, group, leaf_ref, group_ref, end_sems)
        finish(sent)
    over_bands(rows // WIDE, lambda k: finish(banded(outgoing, out_sems, k)))


def fit(last, sums, base, along, root, order):
    rows, columns = sums.shape
    rank = root.shape[1]
    state = ((rows, columns), f32)
    scratch = [pltpu.VMEM(*state)] * 2 + [pltpu.VMEM(along.shape, bf16)]
    sems = [DMA((4, rows // WIDE)), DMA((2, rows // WIDE))]
    if last:
        outs = [state, state]
        scratch += [pltpu.VMEM((rows, 4 * columns), bf16)]
    else:
        outs = [state, ((rank, columns), f32), ((columns, rank), f32)]
        scratch += [pltpu.VMEM((2 * rank, columns), f32)]
        scratch += [pltpu.VMEM(*out) for out in outs[1:]]
        sems += [DMA((2,))]
    return call(
        functools.partial(fit_kernel, last),
        outs,
        18 * rows * columns * rank,
        sums,
        base,
        along,
        root,
        *((order,) if last else ()),
        in_specs=[HBM] * 3 + [VMEM] * (2 if last else 1),
        near_by=2 if last else 1,
        out_specs=[HBM] * len(outs),
        scratch_shapes=scratch + sems,
    )


def near_kernel(first, *refs):
    old_ref, *refs = refs
    given, refs = refs[: 1 if first else 2], refs[1 if first else 2 :]
    along_ref, *refs = refs
    siblings, refs = refs[:SIDE], refs[SIDE:]
    sum_ref, base_ref, *refs = refs
    if first:
        split_ref, block, *refs = refs
    old, sums, base, leaf, split, ready, *refs = refs
    if not first:
        now, *refs = refs
    in_sems, out_sems, start_sems = refs
    rank = siblings[0].shape[0]
    rows = sums.shape[0]
    outgoing = ((sums, sum_ref), (base, base_ref))
    if first:
        arrived = copies_of((old_ref, old, start_sems.at[0]))
        pairs = ((given[0], block),)
        outgoing += ((split.at[0], split_ref.at[0]), (split.at[1], split_ref.at[1]))
    else:
        arrived = copies_of((given[0], now, start_sems.at[0]))
        pairs = ((given[1].at[0], split.at[0]), (given[1].at[1], split.at[1]), (old_ref, old))
    arrived += copies_of((along_ref.at[:, :, pl.ds(0, rank)], leaf, start_sems.at[1]))
    start(arrived)
    start(banded(pairs, in_sems, 0))
    total = siblings[0][...]
    for ref in siblings[1:]:
        total = total + ref[...]
    total = halves(total)
    finish(arrived[:1])
    ahead = AHEAD + 1 if first else AHEAD
    for k in range(1, ahead):
        start(banded(pairs, in_sems, k))
    ready[0], ready[1] = halves(step_size * old[...] if first else now[...])
    finish(arrived[1:])

    def step(k):
        cut = band(k, TILE)
        if first:
            split[0, cut, :], split[1, cut, :] = halves(block[cut, :])
        weights = step_size * old[cut, :] if first else now[cut, :]
        near = product((split[0, cut, :], split[1, cut, :]), (ready[0], ready[1]))
        sums[cut, :] = near + product((leaf[0, cut, :], leaf[1, cut, :]), total)
        base[cut, :] = weights - step_size * shrink_rate * weights + step_size * old[cut, :]
        start(banded(outgoing, out_sems, k))

    stream(pairs, in_sems, step, ahead)
    over_bands(rows // TILE, lambda k: finish(banded(outgoing, out_sems, k)))


def near_sum(blocks, weights, targets, along, siblings):
    rows, columns = targets.shape
    rank = siblings[0].shape[0]
    first = weights is None
    state = ((rows, columns), f32)
    split = ((2, rows, rows), bf16)
    shapes = [((rows, rows), f32)] if first else []
    shapes += [state] * 3 + [((2, rows, rank), bf16), split, ((2, rows, columns), bf16)]
    shapes += [] if first else [state]
    return call(
        functools.partial(near_kernel, first),
        [state] * 2 + ([split] if first else []),
        6 * rows * rows * columns,
        targets,
        *(() if first else (weights,)),
        blocks,
        along,
        *siblings,
        in_specs=[HBM] * (3 if first else 4) + [VMEM] * SIDE,
        near_by=SIDE - 1,
        out_specs=[HBM] * (3 if first else 2),
        scratch_shapes=[pltpu.VMEM(*shape) for shape in shapes]
        + [DMA((3, rows // TILE)), DMA((4, rows // TILE)), DMA((2,))],
    )


def sibling_kernel(split_ref, *refs):
    parts, (first_ref, *out_refs) = refs[:SIDE], refs[SIDE : 2 * SIDE]
    split, given, sums, in_sems, out_sems = refs[2 * SIDE :]
    rank = parts[0].shape[0]
    rows = [pl.ds(k * rank, rank) for k in range(SIDE)]
    arriving = start(
        copies_of(
            *((part, given.at[cut], in_sems.at[k]) for k, (part, cut) in enumerate(zip(parts, rows))),
            (split_ref, split, in_sems.at[SIDE]),
        )
    )
    finish(arriving[:SIDE])
    coefficients = halves(given[...])
    finish(arriving[SIDE:])
    sums[...] = product((split[0], split[1]), coefficients)
    outs = enumerate((first_ref, *out_refs))
    finish(start(copies_of(*((sums.at[rows[k]], out, out_sems.at[k]) for k, out in outs))))


def sibling_sums(couplings, parts):
    rank, columns = parts[0].shape
    whole = pltpu.VMEM((SIDE * rank, columns), f32)
    return call(
        sibling_kernel,
        [((rank, columns), f32)] * SIDE,
        6 * SIDE * SIDE * rank * rank * columns,
        couplings,
        *parts,
        in_specs=[HBM] + [pl.BlockSpec(memory_space=pl.ANY)] * SIDE,
        near_by=SIDE - 1,
        out_specs=[HBM] * SIDE,
        scratch_shapes=[
            pltpu.VMEM(couplings.shape, bf16),
            whole,
            whole,
            DMA((SIDE + 1,)),
            DMA((SIDE,)),
        ],
    )


def sum_kernel(parts_ref, out_ref):
    total = parts_ref[0]
    for k in range(1, parts_ref.shape[0]):
        total = total + parts_ref[k]
    for k in range(out_ref.shape[0]):
        out_ref[k] = total
    out_ref[lax.axis_index("grp")] = jnp.zeros_like(total)


def sum_copies(parts):
    length = lax.axis_size("grp")
    return call(sum_kernel, [((length, *parts.shape[1:]), f32)], 0, parts, near_by=1)[0]


def root_kernel(split_ref, parts_ref, out_ref):
    groups, _, rank = parts_ref.shape
    parts = jnp.concatenate([parts_ref[k] for k in range(groups)], axis=1)
    couplings = [split_ref[k].reshape(groups * rank, rank) for k in range(2)]
    root = product(halves(parts), couplings)
    for k in range(out_ref.shape[0]):
        out_ref[k] = root


def root_copies(parts, tops):
    groups, share, rank = parts.shape
    outs = [((lax.axis_size("sib"), share, rank), f32)]
    return call(root_kernel, outs, 6 * groups * share * rank * rank, tops, parts, near_by=1)[0]


def shards(targets, leaf_order, near_block, leaf_basis, sibling_coupling, transfer, top_coupling):
    ordering = leaf_order[0]
    _, columns = targets.shape
    rank = transfer.shape[0]
    sibs = lax.axis_size("sib")
    share = columns // sibs
    tree_targets = targets.at[ordering].get(unique_indices=True, mode="promise_in_bounds")
    along, leaf_part, group_part = begin(tree_targets, leaf_basis, transfer)
    own, *sent = arrange(sibling_coupling, top_coupling)
    got = [shifted(block, ahead, 0) for ahead, block in enumerate(sent, 1)]
    row_couplings, top_blocks = couple(top_coupling, own, got)
    blocks = near_block
    weights = None
    for iteration in range(ITERS):
        last = iteration == ITERS - 1
        arrived = exchange(group_part.reshape(sibs, share, rank), "sib")
        parts = [leaf_part] + [shifted(leaf_part, 0, behind) for behind in range(1, SIDE)]
        if iteration == 0:
            tops = [top_blocks] + [shifted(top_blocks, 0, behind) for behind in range(1, SIDE)]
            tops = place(tops)
        group_copies = sum_copies(arrived)
        others = exchange(group_copies, "grp")
        sums = sibling_sums(row_couplings, parts)
        sums = [sums[0]] + [shifted(sums[ahead], -ahead, 0) for ahead in range(1, SIDE)]
        roots = root_copies(others, tops)
        root_whole = exchange(roots, "sib").reshape(columns, rank)
        near, base, *split = near_sum(blocks, weights, tree_targets, along, sums)
        blocks = split[0] if split else blocks
        outs = fit(last, near, base, along, root_whole, leaf_order)
        if not last:
            weights, leaf_part, group_part = outs
    return tuple(outs)


def solution(mesh):
    split = P(("grp", "sib"), None)
    return jax.shard_map(
        shards,
        mesh=mesh,
        in_specs=(split,) * 6 + (P("grp", "sib"),),
        out_specs=(split, split),
        check_vma=False,
    )
```

```python
import functools
import math

import jax
import jax.numpy as jnp
from jax import lax
from jax.experimental import pallas as pl
from jax.experimental.pallas import tpu as pltpu
from jax.sharding import PartitionSpec as P


ITERS = 3
SIDE = 4
TILE = 256
WIDE = 640
AHEAD = 2
VMEM_GRANT = 34 << 20

step_size = 0.5
shrink_rate = 0.1
f32, bf16 = jnp.float32, jnp.bfloat16


def halves(value):
    high = value.astype(bf16)
    return high, (value - high.astype(f32)).astype(bf16)


def product(left, right):
    dot = functools.partial(jnp.dot, preferred_element_type=f32)
    return dot(left[0], right[0]) + (dot(left[0], right[1]) + dot(left[1], right[0]))


def call(kernel, outs, flops, *args, near_by=0, **kwargs):
    far = len(args) - near_by
    moved = sum(v.size * v.dtype.itemsize for v in args)
    moved += sum(math.prod(shape) * jnp.dtype(kind).itemsize for shape, kind in outs)
    outs = [pltpu.HBM(*out) for out in outs]
    args = [pltpu.with_memory_space_constraint(v, pltpu.HBM) for v in args[:far]] + [*args[far:]]
    return pl.pallas_call(
        kernel,
        out_shape=outs,
        cost_estimate=pl.CostEstimate(flops=flops, bytes_accessed=moved, transcendentals=0),
        compiler_params=pltpu.CompilerParams(vmem_limit_bytes=VMEM_GRANT),
        **kwargs,
    )(*args)


def exchange(copies, axis):
    return lax.all_to_all(copies, axis, split_axis=0, concat_axis=0, tiled=True)


def shifted(value, rows, columns):
    pairs = [
        (r * SIDE + c, (r + rows) % SIDE * SIDE + (c + columns) % SIDE)
        for r in range(SIDE)
        for c in range(SIDE)
    ]
    return lax.ppermute(value, "sib", pairs)


def sibling_behind(rows, columns):
    sib = lax.axis_index("sib")
    row = lax.rem(sib // SIDE + SIDE - rows, SIDE)
    return row * SIDE + lax.rem(sib % SIDE + SIDE - columns, SIDE)


def arrange_kernel(row_ref, top_ref, own_ref, *sent_refs):
    rank = row_ref.shape[0]
    for ahead in range(SIDE):
        target = own_ref if ahead == 0 else sent_refs[ahead - 1]
        for behind in range(SIDE):
            spot = slice(behind * rank, (behind + 1) * rank)
            if ahead == 0 and behind == 0:
                target[:, spot] = jnp.zeros((rank, rank), f32)
            else:
                source = sibling_behind(SIDE - ahead, behind) if ahead else sibling_behind(0, behind)
                target[:, spot] = row_ref[:, pl.ds(pl.multiple_of(source * rank, rank), rank)]
        if ahead:
            target[:, SIDE * rank :] = top_ref[...]


def arrange(sibling_row, top_block):
    rank = top_block.shape[0]
    wide = ((rank, (SIDE + 1) * rank), f32)
    outs = [((rank, SIDE * rank), f32)] + [wide] * (SIDE - 1)
    return call(arrange_kernel, outs, 0, sibling_row, top_block)


def couple_kernel(top_ref, own_ref, *refs):
    *got, split_ref, tops_ref = refs
    rank = top_ref.shape[0]
    tops_ref[0] = top_ref[...]
    for above in range(SIDE):
        rows = slice(above * rank, (above + 1) * rank)
        block = own_ref[...] if above == 0 else got[above - 1][:, : SIDE * rank]
        split_ref[0, rows, :], split_ref[1, rows, :] = halves(block)
        if above:
            tops_ref[above] = got[above - 1][:, SIDE * rank :]


def couple(top_block, own, got):
    rank = top_block.shape[0]
    outs = [((2, SIDE * rank, SIDE * rank), bf16), ((SIDE, rank, rank), f32)]
    return call(couple_kernel, outs, 0, top_block, own, *got, near_by=SIDE - 1)


def place_kernel(*refs):
    *parts, out_ref = refs
    for behind in range(SIDE):
        for above in range(SIDE):
            owner = sibling_behind(above, behind)
            out_ref[0, owner], out_ref[1, owner] = halves(parts[behind][above].T)


def place(parts):
    _, rank, width = parts[0].shape
    return call(place_kernel, [((2, SIDE * SIDE, rank, width), bf16)], 0, *parts, near_by=SIDE - 1)[0]


def band(index, tile):
    return pl.ds(pl.multiple_of(index * tile, tile), tile)


def over_bands(count, body):
    lax.fori_loop(0, count, lambda k, _: body(k), None)


def copies_of(*ends):
    return [pltpu.make_async_copy(*end) for end in ends]


def start(copies):
    for copy in copies:
        copy.start()
    return copies


def finish(copies):
    for copy in copies:
        copy.wait()


def banded(pairs, sems, index):
    tile = pairs[0][0].shape[0] // sems.shape[1]
    cut = band(index, tile)
    return copies_of(*((a.at[cut], b.at[cut], sems.at[n, index]) for n, (a, b) in enumerate(pairs)))


def lead(pairs, sems):
    for k in range(min(AHEAD, sems.shape[1])):
        start(banded(pairs, sems, k))


def stream(pairs, sems, body, ahead=AHEAD):
    def step(k):
        @pl.when(k + ahead < sems.shape[1])
        def _():
            start(banded(pairs, sems, k + ahead))

        finish(banded(pairs, sems, k))
        body(k)

    over_bands(sems.shape[1], step)


def add_up(total_ref, basis, weights):
    dot = functools.partial(
        lax.dot_general, dimension_numbers=(((0,), (0,)), ((), ())), preferred_element_type=f32
    )
    part = dot(basis[0], weights[0]) + (dot(basis[0], weights[1]) + dot(basis[1], weights[0]))
    total_ref[...] += part


def send_up(total_ref, leaf, group, leaf_ref, group_ref, sems):
    rank = leaf.shape[0]
    leaf[...] = total_ref[:rank, :]
    group[...] = total_ref[rank:, :].T
    return start(copies_of((leaf, leaf_ref, sems.at[0]), (group, group_ref, sems.at[1])))


HBM = pl.BlockSpec(memory_space=pltpu.HBM)
VMEM = pl.BlockSpec(memory_space=pltpu.VMEM)
DMA = pltpu.SemaphoreType.DMA


def begin_kernel(targets_ref, basis_ref, transfer_ref, *refs):
    split_ref, leaf_ref, group_ref, targets, basis, split, total, leaf, group, *sems = refs
    in_sems, out_sems, end_sems = sems
    rows = basis.shape[0]
    pairs = ((targets_ref, targets), (basis_ref, basis))
    outgoing = ((split.at[0], split_ref.at[0]), (split.at[1], split_ref.at[1]))
    lead(pairs, in_sems)
    transfer = halves(transfer_ref[...])
    total[...] = jnp.zeros_like(total)

    def step(k):
        cut = band(k, WIDE)
        both = jnp.concatenate([basis[cut, :], product(halves(basis[cut, :]), transfer)], axis=1)
        high, low = halves(both)
        split[0, cut, :] = high
        split[1, cut, :] = low
        start(banded(outgoing, out_sems, k))
        add_up(total, (high, low), halves(step_size * targets[cut, :]))

    stream(pairs, in_sems, step)
    sent = send_up(total, leaf, group, leaf_ref, group_ref, end_sems)
    over_bands(rows // WIDE, lambda k: finish(banded(outgoing, out_sems, k)))
    finish(sent)


def begin(tree_targets, basis, transfer):
    rows, columns = tree_targets.shape
    rank = transfer.shape[0]
    outs = [((2, rows, 2 * rank), bf16), ((rank, columns), f32), ((columns, rank), f32)]
    return call(
        begin_kernel,
        outs,
        18 * rows * columns * rank,
        tree_targets,
        basis,
        transfer,
        in_specs=[HBM, HBM, VMEM],
        near_by=1,
        out_specs=[HBM] * 3,
        scratch_shapes=[
            pltpu.VMEM((rows, columns), f32),
            pltpu.VMEM((rows, rank), f32),
            pltpu.VMEM(*outs[0]),
            pltpu.VMEM((2 * rank, columns), f32),
            *(pltpu.VMEM(*out) for out in outs[1:]),
            DMA((2, rows // WIDE)),
            DMA((2, rows // WIDE)),
            DMA((2,)),
        ],
    )


def carried(weights, targets):
    return weights - step_size * shrink_rate * weights + step_size * targets


def fit_kernel(first, last, *refs):
    sum_ref, base_ref, along_ref, root_ref, *refs = refs
    if last:
        order_ref, coeffs_ref, fitted_ref, sums, base, along, split, in_sems, out_sems = refs
        outgoing = ((sums, coeffs_ref), (base, fitted_ref))
    else:
        coeffs_ref, leaf_ref, group_ref, sums, base, along, *refs = refs
        total, leaf, group, in_sems, out_sems, end_sems = refs
        total[...] = jnp.zeros_like(total)
        outgoing = ((base, coeffs_ref),)
    rows, columns = sums.shape
    rank = root_ref.shape[1]
    pairs = ((sum_ref, sums), (base_ref, base))
    pairs += ((along_ref.at[0], along.at[0]), (along_ref.at[1], along.at[1]))
    lead(pairs, in_sems)
    root = halves(root_ref[...].T)

    def step(k):
        cut = band(k, WIDE)
        high, low = along[0, cut, :], along[1, cut, :]
        fitted = jnp.tanh(sums[cut, :] + product((along[0, cut, rank:], along[1, cut, rank:]), root))
        given = base[cut, :]
        if first:
            given = carried(step_size * given, given)
        weights = given - step_size * fitted
        if last:
            for n, part in enumerate((*halves(weights), *halves(fitted))):
                split[cut, n * columns : (n + 1) * columns] = part
        else:
            base[cut, :] = weights
            start(banded(outgoing, out_sems, k))
            add_up(total, (high, low), halves(weights))

    stream(pairs, in_sems, step)
    if last:
        order = order_ref[...]

        def scatter(k):
            cut = band(k, WIDE)
            positions = lax.broadcasted_iota(jnp.int32, (WIDE, rows), 0) + k * WIDE
            chosen = jnp.where(positions == order, 1.0, 0.0).astype(bf16)
            parts = jnp.dot(chosen, split[...], preferred_element_type=f32)
            sums[cut, :] = parts[:, :columns] + parts[:, columns : 2 * columns]
            base[cut, :] = parts[:, 2 * columns : 3 * columns] + parts[:, 3 * columns :]
            start(banded(outgoing, out_sems, k))

        over_bands(rows // WIDE, scatter)
    else:
        sent = send_up(total, leaf, group, leaf_ref, group_ref, end_sems)
        finish(sent)
    over_bands(rows // WIDE, lambda k: finish(banded(outgoing, out_sems, k)))


def fit(first, last, sums, base, along, root, order):
    rows, columns = sums.shape
    rank = root.shape[1]
    state = ((rows, columns), f32)
    scratch = [pltpu.VMEM(*state)] * 2 + [pltpu.VMEM(along.shape, bf16)]
    sems = [DMA((4, rows // WIDE)), DMA((2, rows // WIDE))]
    if last:
        outs = [state, state]
        scratch += [pltpu.VMEM((rows, 4 * columns), bf16)]
    else:
        outs = [state, ((rank, columns), f32), ((columns, rank), f32)]
        scratch += [pltpu.VMEM((2 * rank, columns), f32)]
        scratch += [pltpu.VMEM(*out) for out in outs[1:]]
        sems += [DMA((2,))]
    return call(
        functools.partial(fit_kernel, first, last),
        outs,
        18 * rows * columns * rank,
        sums,
        base,
        along,
        root,
        *((order,) if last else ()),
        in_specs=[HBM] * 3 + [VMEM] * (2 if last else 1),
        near_by=2 if last else 1,
        out_specs=[HBM] * len(outs),
        scratch_shapes=scratch + sems,
    )


def near_kernel(first, *refs):
    old_ref, *refs = refs
    given, refs = refs[: 1 if first else 2], refs[1 if first else 2 :]
    along_ref, *refs = refs
    siblings, (sum_ref, *refs) = refs[:SIDE], refs[SIDE:]
    if first:
        split_ref, block, *refs = refs
    else:
        base_ref, *refs = refs
    old, sums, base, leaf, split, ready, *refs = refs
    if not first:
        now, *refs = refs
    in_sems, out_sems, start_sems = refs
    rank = siblings[0].shape[0]
    rows = sums.shape[0]
    outgoing = ((sums, sum_ref),) if first else ((sums, sum_ref), (base, base_ref))
    if first:
        arrived = copies_of((old_ref, old, start_sems.at[0]))
        pairs = ((given[0], block),)
        outgoing += ((split.at[0], split_ref.at[0]), (split.at[1], split_ref.at[1]))
    else:
        arrived = copies_of((given[0], now, start_sems.at[0]))
        pairs = ((given[1].at[0], split.at[0]), (given[1].at[1], split.at[1]), (old_ref, old))
    arrived += copies_of((along_ref.at[:, :, pl.ds(0, rank)], leaf, start_sems.at[1]))
    start(arrived)
    start(banded(pairs, in_sems, 0))
    total = siblings[0][...]
    for ref in siblings[1:]:
        total = total + ref[...]
    total = halves(total)
    finish(arrived[:1])
    ahead = AHEAD + 1 if first else AHEAD
    for k in range(1, ahead):
        start(banded(pairs, in_sems, k))
    ready[0], ready[1] = halves(step_size * old[...] if first else now[...])
    finish(arrived[1:])

    def step(k):
        cut = band(k, TILE)
        if first:
            split[0, cut, :], split[1, cut, :] = halves(block[cut, :])
        near = product((split[0, cut, :], split[1, cut, :]), (ready[0], ready[1]))
        sums[cut, :] = near + product((leaf[0, cut, :], leaf[1, cut, :]), total)
        if not first:
            base[cut, :] = carried(now[cut, :], old[cut, :])
        start(banded(outgoing, out_sems, k))

    stream(pairs, in_sems, step, ahead)
    over_bands(rows // TILE, lambda k: finish(banded(outgoing, out_sems, k)))


def near_sum(blocks, weights, targets, along, siblings):
    rows, columns = targets.shape
    rank = siblings[0].shape[0]
    first = weights is None
    state = ((rows, columns), f32)
    split = ((2, rows, rows), bf16)
    shapes = [((rows, rows), f32)] if first else []
    shapes += [state] * 3 + [((2, rows, rank), bf16), split, ((2, rows, columns), bf16)]
    shapes += [] if first else [state]
    return call(
        functools.partial(near_kernel, first),
        [state, split] if first else [state] * 2,
        6 * rows * rows * columns,
        targets,
        *(() if first else (weights,)),
        blocks,
        along,
        *siblings,
        in_specs=[HBM] * (3 if first else 4) + [VMEM] * SIDE,
        near_by=SIDE - 1,
        out_specs=[HBM] * 2,
        scratch_shapes=[pltpu.VMEM(*shape) for shape in shapes]
        + [DMA((3, rows // TILE)), DMA((4, rows // TILE)), DMA((2,))],
    )


def sibling_kernel(split_ref, *refs):
    parts, (first_ref, *out_refs) = refs[:SIDE], refs[SIDE : 2 * SIDE]
    split, given, sums, in_sems, out_sems = refs[2 * SIDE :]
    rank = parts[0].shape[0]
    rows = [pl.ds(k * rank, rank) for k in range(SIDE)]
    arriving = start(
        copies_of(
            *((part, given.at[cut], in_sems.at[k]) for k, (part, cut) in enumerate(zip(parts, rows))),
            (split_ref, split, in_sems.at[SIDE]),
        )
    )
    finish(arriving[:SIDE])
    coefficients = halves(given[...])
    finish(arriving[SIDE:])
    sums[...] = product((split[0], split[1]), coefficients)
    outs = enumerate((first_ref, *out_refs))
    finish(start(copies_of(*((sums.at[rows[k]], out, out_sems.at[k]) for k, out in outs))))


def sibling_sums(couplings, parts):
    rank, columns = parts[0].shape
    whole = pltpu.VMEM((SIDE * rank, columns), f32)
    return call(
        sibling_kernel,
        [((rank, columns), f32)] * SIDE,
        6 * SIDE * SIDE * rank * rank * columns,
        couplings,
        *parts,
        in_specs=[HBM] + [pl.BlockSpec(memory_space=pl.ANY)] * SIDE,
        near_by=SIDE - 1,
        out_specs=[HBM] * SIDE,
        scratch_shapes=[
            pltpu.VMEM(couplings.shape, bf16),
            whole,
            whole,
            DMA((SIDE + 1,)),
            DMA((SIDE,)),
        ],
    )


def sum_kernel(parts_ref, out_ref):
    total = parts_ref[0]
    for k in range(1, parts_ref.shape[0]):
        total = total + parts_ref[k]
    for k in range(out_ref.shape[0]):
        out_ref[k] = total
    out_ref[lax.axis_index("grp")] = jnp.zeros_like(total)


def sum_copies(parts):
    length = lax.axis_size("grp")
    return call(sum_kernel, [((length, *parts.shape[1:]), f32)], 0, parts, near_by=1)[0]


def root_kernel(split_ref, parts_ref, out_ref):
    groups, _, rank = parts_ref.shape
    parts = jnp.concatenate([parts_ref[k] for k in range(groups)], axis=1)
    couplings = [split_ref[k].reshape(groups * rank, rank) for k in range(2)]
    root = product(halves(parts), couplings)
    for k in range(out_ref.shape[0]):
        out_ref[k] = root


def root_copies(parts, tops):
    groups, share, rank = parts.shape
    outs = [((lax.axis_size("sib"), share, rank), f32)]
    return call(root_kernel, outs, 6 * groups * share * rank * rank, tops, parts, near_by=1)[0]


def shards(targets, leaf_order, near_block, leaf_basis, sibling_coupling, transfer, top_coupling):
    ordering = leaf_order[0]
    _, columns = targets.shape
    rank = transfer.shape[0]
    sibs = lax.axis_size("sib")
    share = columns // sibs
    tree_targets = targets.at[ordering].get(unique_indices=True, mode="promise_in_bounds")
    along, leaf_part, group_part = begin(tree_targets, leaf_basis, transfer)
    own, *sent = arrange(sibling_coupling, top_coupling)
    got = [shifted(block, ahead, 0) for ahead, block in enumerate(sent, 1)]
    row_couplings, top_blocks = couple(top_coupling, own, got)
    blocks = near_block
    weights = None
    for iteration in range(ITERS):
        last = iteration == ITERS - 1
        arrived = exchange(group_part.reshape(sibs, share, rank), "sib")
        parts = [leaf_part] + [shifted(leaf_part, 0, behind) for behind in range(1, SIDE)]
        if iteration == 0:
            tops = [top_blocks] + [shifted(top_blocks, 0, behind) for behind in range(1, SIDE)]
            tops = place(tops)
        group_copies = sum_copies(arrived)
        others = exchange(group_copies, "grp")
        sums = sibling_sums(row_couplings, parts)
        sums = [sums[0]] + [shifted(sums[ahead], -ahead, 0) for ahead in range(1, SIDE)]
        roots = root_copies(others, tops)
        root_whole = exchange(roots, "sib").reshape(columns, rank)
        first = iteration == 0
        near, other = near_sum(blocks, weights, tree_targets, along, sums)
        base, blocks = (tree_targets, other) if first else (other, blocks)
        outs = fit(first, last, near, base, along, root_whole, leaf_order)
        if not last:
            weights, leaf_part, group_part = outs
    return tuple(outs)


def solution(mesh):
    split = P(("grp", "sib"), None)
    return jax.shard_map(
        shards,
        mesh=mesh,
        in_specs=(split,) * 6 + (P("grp", "sib"),),
        out_specs=(split, split),
        check_vma=False,
    )
```
